256 devices in a mesh: ens: 4 (over y), tile: 64 (over x, z, core).
Axes of the slice: x: 4, y: 4, z: 8, core: 2. Of those that a mesh axis runs over, the one named last changes fastest.
Arguments:
- surface: float32 [65536, 1024], P(('ens', 'tile')), parts along dimension 0, may hold values from -6 to 6
- flux_x: float32 [65536, 1024], P(('ens', 'tile')), parts along dimension 0, may hold values from -3 to 3
- flux_y: float32 [65536, 1024], P(('ens', 'tile')), parts along dimension 0, may hold values from -3 to 3
- celerity: float32 [65536, 1024], P(('ens', 'tile')), parts along dimension 0, may hold values from 0.05 to 0.45
- bed_depth: float32 [65536, 1024], P(('ens', 'tile')), parts along dimension 0, may hold values from 0.2 to 3
- roughness: float32 [65536, 1024], P(('ens', 'tile')), parts along dimension 0, may hold values from 0.2 to 2
- smoother: bfloat16 [256, 256], replicated, may hold values from -0.5 to 1.5
- block_plan: int32 [256, 4], P(('ens', 'tile')), parts along dimension 0, may hold values from 0 to 3, as said below
Outputs:
- new_surface: float32 [65536, 1024], P(('ens', 'tile')), parts along dimension 0
- new_flux_x: float32 [65536, 1024], P(('ens', 'tile')), parts along dimension 0
- new_flux_y: float32 [65536, 1024], P(('ens', 'tile')), parts along dimension 0
- resident: float32 [768, 2, 256, 256], P(('ens', 'tile')), parts along dimension 0
- energy: float32 [8], P('ens'), parts along dimension 0
The draws below stay inside these ranges and needn't reach their ends.
There are 4 independent parts, one for each index of `ens`. The reference program is written for one: setup_inputs(seed, part) draws one part's arguments, and reference() takes and returns one part's arrays. A program takes and returns all parts, laid end to end along the dimension named above; an argument that names none is the same for every part. Nothing has to cross between parts.
Inputs may be any that keep to these rules, and one draw needn't show every extreme that they name: `block_plan`: codes per block: 0 dry, 1 to 3 wet with the slots of the steps. Every tile holds exactly one block of each code 1, 2 and 3 and one dry block, so every slot holds exactly one block.
All inputs are finite; a program needn't handle non-finite values.
Results may differ from the reference program's by a relative error of at most 0.022.
Values may be sent and summed in bfloat16 or wider, within the bound.
No kernel may reach another device: no remote copies, remote signals or barrier semaphores. Data moves between devices by JAX's collectives and lax.ppermute only.
A program may use at most 64 MiB of HBM per device.

```python
import math
import jax
import jax.numpy as jnp
from jax import lax

B = 256
BPD = 4
STEPS = 2
SUB = 12
RSLOT = 3
NC = 1024
NX = 16384
N_TILE = 64


def draw_smoother(key, part):
    noise = jax.random.normal(key, (B, B), jnp.float32)
    return (jnp.eye(B, dtype=jnp.float32) + noise * (0.3 / math.sqrt(B))).astype(jnp.bfloat16)


def draw_block_plan(key, part):
    spots = jnp.arange(BPD, dtype=jnp.int32)
    scores = jax.random.randint(key, (N_TILE, BPD), 0, 2 ** 20) * BPD + spots[None, :]
    ranks = jnp.argsort(scores, axis=1).astype(jnp.int32)
    codes = jnp.where(ranks < 4, ranks, 0).astype(jnp.int32)
    return codes.astype(jnp.int32)


def level_of(own_key, dims, split, low, largest):
    def one(dim, blocks):
        steps = jax.random.uniform(jax.random.fold_in(jax.random.fold_in(own_key, 6), dim), (blocks,), jnp.float32, low / len(split), largest / len(split))
        return jnp.repeat(jnp.exp(steps), dims[dim] // blocks).reshape((-1,) + (1,) * (len(dims) - dim - 1))

    factor_of = one(*split[0])
    for cut in split[1:]:
        factor_of = factor_of * one(*cut)
    return factor_of


def scatter_about(key, shape, deviation, reach, cuts=(), kind=jnp.bfloat16):
    drawn = jax.random.normal(key, shape, jnp.float32) * deviation
    if len(cuts) > 0:
        drawn = level_of(key, shape, cuts, -0.22, 0.18) * drawn
    return jnp.clip(drawn, min=-reach, max=reach).astype(kind)


def setup_inputs(seed: int = 0, part: int = 0) -> dict:
    splits = jax.random.split(jax.random.key(seed), 9)
    part_splits = jax.random.split(jax.random.fold_in(splits[8], part), 9)
    return {
        "surface": scatter_about(part_splits[0], (NX, NC), 1.0, 6.0, ((0, 64),), jnp.float32),
        "flux_x": scatter_about(part_splits[1], (NX, NC), 0.5, 3.0, ((0, 64),), jnp.float32),
        "flux_y": scatter_about(part_splits[2], (NX, NC), 0.5, 3.0, ((0, 64),), jnp.float32),
        "celerity": jnp.clip(jnp.exp(math.log(0.45) - 2.1972245 * jax.random.uniform(part_splits[3], (NX, NC), jnp.float32) ** level_of(part_splits[3], (NX, NC), ((0, 64),), -0.2, 0.2)), 0.05, 0.45),
        "bed_depth": jnp.clip(0.2 + 2.8 * jax.random.uniform(part_splits[4], (NX, NC), jnp.float32) ** level_of(part_splits[4], (NX, NC), ((0, 64),), -0.2, 0.2), 0.2, 3.0),
        "roughness": jnp.clip(jnp.exp(math.log(2.0) - 2.3025851 * jax.random.uniform(part_splits[5], (NX, NC), jnp.float32) ** level_of(part_splits[5], (NX, NC), ((0, 64),), -0.2, 0.2)), 0.2, 2.0),
        "smoother": draw_smoother(jax.random.fold_in(splits[8], 71), part),
        "block_plan": draw_block_plan(jax.random.fold_in(jax.random.fold_in(splits[8], part), 71), part),
    }


def to_blocks(field, tiles):
    return field.reshape(tiles, B, BPD, B).transpose(0, 2, 1, 3).reshape(tiles * BPD, B, B)


def from_blocks(blocks, tiles):
    return blocks.reshape(tiles, BPD, B, B).transpose(0, 2, 1, 3).reshape(tiles * B, BPD * B)


def settle_slot(held, drag_ratio, smoother):
    weight = drag_ratio.astype(jnp.float32)
    wide = smoother.astype(jnp.float32)
    settled = jnp.zeros(held.shape, jnp.float32)
    for _ in range(SUB):
        partial_rows = jnp.einsum("fij,kj->fik", held.astype(jnp.float32), wide).astype(jnp.bfloat16)
        mixed_full = jnp.einsum("ki,fij->fkj", wide, partial_rows.astype(jnp.float32))
        settled = mixed_full / (1.0 + weight * jnp.abs(mixed_full))
        held = settled.astype(jnp.bfloat16)
    return settled


def reference(surface, flux_x, flux_y, celerity, bed_depth, roughness, smoother, block_plan):
    row_total, col_total = surface.shape
    tiles = row_total // B
    half_cols = col_total // 2
    col_ids = jnp.arange(col_total, dtype=jnp.int32)
    right_edge = (col_ids % half_cols == half_cols - 1)[None, :]
    left_edge = (col_ids % half_cols == 0)[None, :]
    level, flow_x, flow_y = surface, flux_x, flux_y
    zero_row = jnp.zeros((1, col_total), jnp.float32)
    wet_flags = (block_plan > 0).reshape(-1)
    tile_ids = jnp.arange(tiles, dtype=jnp.int32)[:, None]
    dest_slot = (block_plan - 1).astype(jnp.int32)
    dest_tile = (tile_ids + dest_slot) % tiles
    target = (dest_tile * RSLOT + dest_slot).reshape(-1).astype(jnp.int32)
    slot_ids = jnp.arange(tiles * RSLOT, dtype=jnp.int32)
    block_ids = jnp.arange(tiles * BPD, dtype=jnp.int32)
    matches = (target[:, None] == slot_ids[None, :]) & wet_flags[:, None]
    source = jnp.sum(jnp.where(matches, block_ids[:, None], 0), axis=0).astype(jnp.int32)
    filled = jnp.any(matches, axis=0)
    safe_target = jnp.where(wet_flags, target, 0).astype(jnp.int32)

    def settle_pair(pair):
        return settle_slot(pair[0], pair[1], smoother)

    resident = jnp.zeros((tiles * RSLOT, 2, B, B), jnp.float32)
    for repeat in range(STEPS):
        ahead_rows = jnp.concatenate([level[1:], zero_row], 0)
        flow_x = flow_x - celerity * (ahead_rows - level)
        right_cells = jnp.where(right_edge, 0.0, jnp.roll(level, -1, axis=1))
        flow_y = flow_y - celerity * (right_cells - level)
        behind_x = jnp.concatenate([zero_row, flow_x[:-1]], 0)
        behind_y = jnp.where(left_edge, 0.0, jnp.roll(flow_y, 1, axis=1))
        level = level - (flow_x - behind_x) - (flow_y - behind_y)
        drag_full = (roughness / jnp.maximum(level + bed_depth, 1.0)).astype(jnp.bfloat16)
        flow_blocks = jnp.stack([to_blocks(flow_x, tiles), to_blocks(flow_y, tiles)], 1)
        drag_blocks = to_blocks(drag_full, tiles)
        held = jnp.where(filled[:, None, None, None], flow_blocks[source], 0.0).astype(jnp.bfloat16)
        drag_held = jnp.where(filled[:, None, None], drag_blocks[source], jnp.zeros((), drag_blocks.dtype))
        resident = lax.map(settle_pair, (held, drag_held))
        updated = jnp.where(wet_flags[:, None, None, None], resident[safe_target], flow_blocks)
        flow_x = from_blocks(updated[:, 0], tiles)
        flow_y = from_blocks(updated[:, 1], tiles)
    row_weight = 1.0 + 2.0 * jnp.arange(row_total, dtype=jnp.float32) / row_total
    squares = (row_weight[:, None] * level * level).reshape(row_total, 2, half_cols)
    energy = jnp.sum(squares, axis=(0, 2)) / (row_total * half_cols)
    return level, flow_x, flow_y, resident, energy
```

```python
import jax
import jax.numpy as jnp
from jax import lax
from jax.experimental import pallas as pl
from jax.experimental.pallas import tpu as pltpu
from jax.sharding import PartitionSpec as P

SUB = 12
EARLY = 6
EDGE = 8
PACK = 16
BAND = 32
GRANT = 16 * 2**20
F32 = jnp.float32
BF16 = jnp.bfloat16
VMEM = pl.BlockSpec(memory_space=pltpu.VMEM)
SMEM = pl.BlockSpec(memory_space=pltpu.SMEM)
HBM = pl.BlockSpec(memory_space=pltpu.HBM)


def shifted_left(rows, half):
    cols = rows.shape[1]
    ids = lax.broadcasted_iota(jnp.int32, rows.shape, 1) % half
    return jnp.where(ids == half - 1, 0.0, pltpu.roll(rows, cols - 1, 1))


def shifted_right(rows, half):
    ids = lax.broadcasted_iota(jnp.int32, rows.shape, 1) % half
    return jnp.where(ids == 0, 0.0, pltpu.roll(rows, 1, 1))


def drag_of(rough, level, depth):
    return (rough / jnp.maximum(level + depth, 1.0)).astype(BF16)


def code_column(plan, code, side):
    column = 0
    for k in range(plan.shape[1]):
        column = column + jnp.where(plan[0, k] == code, k * side, 0)
    return pl.multiple_of(column, side)


def advance(half, level, ahead, flow_x, flow_y, celerity, above_x):
    rows = level.shape[0]
    row_ids = lax.broadcasted_iota(jnp.int32, level.shape, 0)
    below = jnp.where(row_ids == rows - 1, ahead, pltpu.roll(level, rows - 1, 0))
    new_x = flow_x - celerity * (below - level)
    new_y = flow_y - celerity * (shifted_left(level, half) - level)
    behind_x = jnp.where(row_ids == 0, above_x, pltpu.roll(new_x, 1, 0))
    new_level = level - (new_x - behind_x) - (new_y - shifted_right(new_y, half))
    return new_x, new_y, new_level


def edge_rows(s, x, y, c, up, down, first, heads, tails, sems):
    rows = s.shape[0]
    copies = []
    for j, array in enumerate((s, x, y, c)):
        copies.append(pltpu.make_async_copy(array.at[pl.ds(0, EDGE)], heads.at[j], sems.at[2 * j]))
        copies.append(pltpu.make_async_copy(array.at[pl.ds(rows - EDGE, EDGE)], tails.at[j], sems.at[2 * j + 1]))
    for copy in copies:
        copy.start()
    for copy in copies:
        copy.wait()
    up[0:2] = heads[0, 0:2]
    for j in range(1, 4):
        up[j + 1:j + 2] = heads[j, 0:1]
    down[0:2] = tails[0, EDGE - 2:]
    down[2:4] = tails[1, EDGE - 2:]
    down[4:6] = tails[3, EDGE - 2:]
    down[6:7] = tails[2, EDGE - 1:]
    first[...] = heads[0, 0:1]


def first_step(s_in, x_in, y_in, c_in, b_in, r_in, sm_in, x_out, y_out, l_out, d_out, c, b, r, sm, sm_t,
               s, x, y, sems, sm_sem):
    total, cols = s.shape
    half = cols // 2
    bands = total // BAND
    pairs = ((s_in, s), (c_in, c), (x_in, x), (y_in, y), (b_in, b), (r_in, r))

    def copy(i, j):
        rows = pl.ds(i * BAND, BAND)
        source, target = pairs[j]
        return pltpu.make_async_copy(source.at[rows], target.at[rows], sems.at[i, j])

    sm_copy = pltpu.make_async_copy(sm_in, sm, sm_sem)
    sm_copy.start()
    for i in range(bands):
        for j in range(len(pairs)):
            copy(i, j).start()
    sm_copy.wait()
    sm_t[...] = sm[...].T
    above = jnp.zeros((1, cols), F32)
    for j in range(len(pairs)):
        copy(0, j).wait()
    for i in range(bands):
        rows = pl.ds(i * BAND, BAND)
        if i + 1 < bands:
            for j in range(len(pairs)):
                copy(i + 1, j).wait()
            ahead = s[pl.ds((i + 1) * BAND, 1)]
        else:
            ahead = jnp.zeros((1, cols), F32)
        new_x, new_y, level = advance(half, s[rows], ahead, x[rows], y[rows], c[rows], above)
        above = new_x[BAND - 1:]
        x_out[rows] = new_x
        y_out[rows] = new_y
        l_out[rows] = level
        d_out[rows] = drag_of(r[rows], level, b[rows])


def row_weight(shape, start, total_rows):
    ids = lax.broadcasted_iota(jnp.int32, shape, 0) + start
    return 1.0 + ids.astype(F32) * (2.0 / total_rows)


def second_step(tile_count, l_in, l_head, l_tail, halo, x_in, y_in, c, b, r, x_out, y_out, l_out, d_out, sums_out):
    total, cols = l_in.shape
    half = cols // 2
    bands = total // BAND
    position = lax.axis_index("tile")

    def level_band(i):
        start, stop = i * BAND, (i + 1) * BAND
        parts = [l_in[pl.ds(start, BAND)]]
        if i == 0:
            parts = [l_head[...], l_in[pl.ds(EDGE, BAND - EDGE)]]
        if i == bands - 1:
            parts = [l_in[pl.ds(start, BAND - EDGE)], l_tail[...]]
        return jnp.concatenate(parts, 0)

    above = jnp.zeros((1, cols), F32)
    sums = jnp.zeros((EDGE, cols), F32)
    level = level_band(0)
    for i in range(bands):
        rows = pl.ds(i * BAND, BAND)
        following = level_band(i + 1) if i + 1 < bands else halo[...]
        new_x, new_y, new_level = advance(half, level, following[0:1], x_in[rows], y_in[rows], c[rows], above)
        level = following
        above = new_x[BAND - 1:]
        x_out[rows] = new_x
        y_out[rows] = new_y
        l_out[rows] = new_level
        d_out[rows] = drag_of(r[rows], new_level, b[rows])
        for j in range(BAND // EDGE):
            if i + j > 0:
                part = new_level[j * EDGE:(j + 1) * EDGE]
                weight = row_weight(part.shape, position * total + i * BAND + j * EDGE, tile_count * total)
                sums = sums + weight * (part * part)
    sums_out[...] = sums


def second_edge(tile_count, row_count, down, halo, l_head, l2_head, sums, b_head, r_head, head, d_head, shares):
    cols = l_head.shape[1]
    half = cols // 2
    position = lax.axis_index("tile")
    total_rows = tile_count * row_count
    has_previous = jnp.where(position == 0, 0.0, 1.0)
    above_x = has_previous * (down[...] - halo[2:3] * (l_head[0:1] - halo[1:2]))
    row_ids = lax.broadcasted_iota(jnp.int32, (PACK, cols), 0)
    level = l2_head[...] + jnp.where(row_ids == 0, above_x, 0.0)
    head[...] = level
    d_head[...] = drag_of(r_head[...], level, b_head[...])
    top = level[:EDGE]
    whole = sums[...] + row_weight(top.shape, position * row_count, total_rows) * (top * top)
    lanes = lax.broadcasted_iota(jnp.int32, (1, 128), 1)
    share = jnp.zeros((1, 128), F32)
    for scenario in range(2):
        part = whole[:, scenario * half:(scenario + 1) * half]
        share = jnp.where(lanes == 2 * position + scenario, jnp.sum(part) * (1.0 / (total_rows * half)), share)
    shares[...] = share


def soften(smooth, smooth_t, held, drags, chains, repeats, put=None):
    for repeat in range(repeats):
        for chain in range(chains):
            mixed = jnp.dot(held[chain], smooth_t, preferred_element_type=F32).astype(BF16)
            full = jnp.dot(smooth, mixed, preferred_element_type=F32)
            settled = full / (1.0 + drags[chain // 2].astype(F32) * jnp.abs(full))
            if put is None or repeat + 1 < repeats:
                held[chain] = settled.astype(BF16)
            else:
                put(chain, settled)


def smooth_all(tile_count, plan, up, down, first, c, b, r, sm, sm_t, x_in, y_in, l_in, d_in,
               x, y, l_head, l_tail, halo, x_last, held, drags, edge):
    rows, cols = x.shape
    half = cols // 2
    side = sm.shape[0]
    position = lax.axis_index("tile")
    has_next = jnp.where(position == tile_count - 1, 0.0, 1.0)
    has_previous = jnp.where(position == 0, 0.0, 1.0)
    below = up[...] * has_next
    above = down[...] * has_previous
    tail, head = pl.ds(rows - EDGE, EDGE), pl.ds(0, EDGE)
    row_ids = lax.broadcasted_iota(jnp.int32, (EDGE, cols), 0)
    own_first = first[...]

    change = jnp.where(row_ids == EDGE - 1, c[tail] * below[0:1], 0.0)
    x_tail = x_in[tail] - change
    low = l_in[tail] + change
    l_tail[...] = low
    above_x = above[3:4] - above[5:6] * (own_first - above[1:2])
    top = l_in[head] + jnp.where(row_ids == 0, above_x, 0.0)
    l_head[...] = top

    next_x = below[2:3] - below[4:5] * (below[1:2] - below[0:1])
    next_y = below[3:4] - below[4:5] * (shifted_left(below[0:1], half) - below[0:1])
    next_level = below[0:1] - (next_x - x_tail[EDGE - 1:]) - (next_y - shifted_right(next_y, half))
    halo[0:1] = has_next * next_level
    before_x = above[2:3] - above[4:5] * (above[1:2] - above[0:1])
    before_y = above[6:7] - above[5:6] * (shifted_left(above[1:2], half) - above[1:2])
    halo[1:2] = above[1:2] - (above_x - before_x) - (before_y - shifted_right(before_y, half))
    halo[2:3] = above[5:6]

    first_rows, last_rows = pl.ds(0, PACK), pl.ds(rows - PACK, PACK)
    first_edge, last_edge = pl.ds(0, PACK), pl.ds(PACK, PACK)
    edge[first_edge] = drag_of(r[first_rows], jnp.concatenate([top, l_in[pl.ds(EDGE, EDGE)]], 0), b[first_rows])
    edge[last_edge] = drag_of(r[last_rows], jnp.concatenate([l_in[pl.ds(rows - PACK, EDGE)], low], 0), b[last_rows])
    x[...] = x_in[...]
    x[tail] = x_tail
    y[...] = y_in[...]
    columns = [code_column(plan, code, side) for code in (1, 2, 3)]
    for slot, column in enumerate(columns):
        span = pl.ds(column, side)
        drags[slot] = d_in[:, span]
        drags[slot, first_rows] = edge[first_edge, span]
        drags[slot, last_rows] = edge[last_edge, span]
        held[2 * slot] = x[:, span].astype(BF16)
        held[2 * slot + 1] = y[:, span].astype(BF16)

    def put(chain, settled):
        flux = (x, y)[chain % 2]
        flux[:, pl.ds(columns[chain // 2], side)] = settled

    soften(sm[...], sm_t[...], held, drags, 6, SUB, put)
    x_last[...] = x[rows - 1:rows]


def start_blocks(codes, plan, x, y, d, d_head, sm, sm_t, held, drags, edge):
    side = sm.shape[0]
    edge[...] = d_head[...]
    for slot, code in enumerate(codes):
        span = pl.ds(code_column(plan, code, side), side)
        drags[slot] = d[:, span]
        drags[slot, 0:PACK] = edge[:, span]
        held[2 * slot] = x[:, span].astype(BF16)
        held[2 * slot + 1] = y[:, span].astype(BF16)
    soften(sm[...], sm_t[...], held, drags, 2 * len(codes), EARLY)


def finish_sent(sm, sm_t, held_in, drags, settled_out, near, far, held):
    held[...] = held_in[...]

    def put(chain, settled):
        settled_out[chain // 2, chain % 2] = settled
        (near, far)[chain // 2][chain % 2] = settled.astype(BF16)

    soften(sm[...], sm_t[...], held, drags, 4, SUB - EARLY, put)


def finish_own(plan, sm, sm_t, held_in, drags, x_in, y_in, l_in, head, sent, x, y, lev, resident, held, stage, sems):
    side = sm.shape[0]
    rows = l_in.shape[0]
    blocks = plan.shape[1]
    places = [(code, pl.ds(code_column(plan, code, side), side)) for code in range(blocks)]
    outs = (x, y)
    copies = [
        (head.at[pl.ds(0, PACK)], lev.at[pl.ds(0, PACK)]),
        (l_in.at[pl.ds(PACK, rows - PACK)], lev.at[pl.ds(PACK, rows - PACK)]),
    ]
    late = [(stage, resident.at[0])]
    for code, span in places:
        for f in range(2):
            target = outs[f].at[:, span]
            if code == 0:
                copies.append(((x_in, y_in)[f].at[:, span], target))
            elif code == 1:
                late.append((stage.at[f], target))
            else:
                copies.append((sent.at[code - 2, f], target))
    started = [pltpu.make_async_copy(a, b, sems.at[i]) for i, (a, b) in enumerate(copies)]
    for copy in started:
        copy.start()
    held[...] = held_in[...]

    def put(chain, settled):
        stage[chain] = settled

    soften(sm[...], sm_t[...], held, drags, 2, SUB - EARLY, put)
    for i, (a, b) in enumerate(late):
        started.append(pltpu.make_async_copy(a, b, sems.at[len(copies) + i]))
        started[-1].start()
    for copy in started:
        copy.wait()


def settle_resident(near, far, held_resident, resident, stage, sems):
    copies = []
    for slot, block in enumerate((near, far)):
        stage[slot] = block[...].astype(F32)
        copies.append(pltpu.make_async_copy(stage.at[slot], resident.at[slot + 1], sems.at[slot]))
        copies[-1].start()
    for copy in copies:
        copy.wait()


def add_shares(mine, received, energy):
    shares = mine[...] + received[...]
    lanes = lax.broadcasted_iota(jnp.int32, shares.shape, 1)
    for scenario in range(2):
        energy[scenario] = jnp.sum(jnp.where(lanes % 2 == scenario, shares, 0.0))


def moved(value, steps):
    count = lax.axis_size("tile")
    return lax.ppermute(value, "tile", [(i, (i + steps) % count) for i in range(count)])


def exchange_stages(count):
    deep = 8 if count >= 16 else max(count // 2, 1)
    wide = count // (2 * deep)

    def index(x, z, core):
        return (x * deep + z) * 2 + core

    def stage(rule):
        pairs = []
        for i in range(count):
            core, z, x = i % 2, (i // 2) % deep, i // (2 * deep)
            pairs.append((i, index(*rule(x, z, core))))
        return pairs

    stages = []
    if deep == 8:
        across = {0: 6, 1: 7, 2: 4, 3: 5, 4: 2, 5: 3, 6: 0, 7: 1}
        stages.append(stage(lambda x, z, core: (x, z ^ 2, core)))
        stages.append(stage(lambda x, z, core: (x, z ^ 1, core)))
    else:
        reach = 1
        while reach < deep:
            stages.append(stage(lambda x, z, core, reach=reach: (x, z ^ reach, core)))
            reach *= 2
    if wide >= 2:
        stages.append(stage(lambda x, z, core: (x ^ 1, z, core)))
    if wide == 4:
        stages.append(stage(lambda x, z, core: (3 - x, z, core)))
    stages.append(stage(lambda x, z, core: (x, z, 1 - core)))
    if deep == 8:
        stages.append(stage(lambda x, z, core: (x, across[z], core)))
    return stages


def on_device(surface, flux_x, flux_y, celerity, bed_depth, roughness, smoother, plan):
    rows, cols = surface.shape
    side = smoother.shape[0]
    tiles = lax.axis_size("tile")

    def arr(*shape, dtype=F32):
        return jax.ShapeDtypeStruct(shape, dtype)

    field, square = arr(rows, cols), arr(side, side, dtype=BF16)
    drag = arr(rows, cols, dtype=BF16)

    def call(body, name, ins, outs, out_specs, operands, scratch=(), aliases={}, flops=0, moved_bytes=0):
        return pl.pallas_call(
            body,
            out_shape=outs,
            in_specs=ins,
            out_specs=out_specs,
            scratch_shapes=scratch,
            input_output_aliases=aliases,
            compiler_params=pltpu.CompilerParams(vmem_limit_bytes=GRANT),
            cost_estimate=pl.CostEstimate(flops=flops, bytes_accessed=moved_bytes, transcendentals=0),
            name=name,
        )(*operands)

    def dots(chains, repeats):
        return chains * repeats * 4 * side**3

    def squares(count):
        return pltpu.VMEM((count, side, side), BF16)

    def partner(value, pairs):
        return lax.ppermute(value, "tile", pairs)

    surface, flux_x, flux_y, celerity, bed_depth, roughness, smoother = [
        pltpu.with_memory_space_constraint(array, pltpu.HBM)
        for array in (surface, flux_x, flux_y, celerity, bed_depth, roughness, smoother)
    ]
    up, down, first = call(
        edge_rows, "edge_rows", [HBM] * 4, (arr(5, cols), arr(7, cols), arr(1, cols)), [VMEM] * 3,
        (surface, flux_x, flux_y, celerity),
        [pltpu.VMEM((4, EDGE, cols), F32)] * 2 + [pltpu.SemaphoreType.DMA((8,))])
    up = moved(up, -1)
    down = moved(down, 1)
    x, y, lev, d, c, b, r, sm, sm_t = call(
        first_step, "first_step", [HBM] * 7, (field, field, field, drag, field, field, field, square, square), [VMEM] * 9,
        (surface, flux_x, flux_y, celerity, bed_depth, roughness, smoother),
        [pltpu.VMEM((rows, cols), F32)] * 3 + [pltpu.SemaphoreType.DMA((rows // BAND, 6)), pltpu.SemaphoreType.DMA],
        flops=20 * rows * cols, moved_bytes=24 * rows * cols)
    x, y, l_head, l_tail, halo, x_last = call(
        lambda *refs: smooth_all(tiles, *refs), "smooth_all", [SMEM] + [VMEM] * 12,
        (field, field, arr(EDGE, cols), arr(EDGE, cols), arr(3, cols), arr(1, cols)), [VMEM] * 6,
        (plan, up, down, first, c, b, r, sm, sm_t, x, y, lev, d),
        [squares(6), squares(3), pltpu.VMEM((2 * PACK, cols), BF16)], flops=dots(6, SUB), moved_bytes=8 * rows * cols)
    down = moved(x_last, 1)
    x, y, lev, d, sums = call(
        lambda *refs: second_step(tiles, *refs), "second_step", [VMEM] * 9,
        (field, field, field, drag, arr(EDGE, cols)), [VMEM] * 5,
        (lev, l_head, l_tail, halo, x, y, c, b, r),
        flops=20 * rows * cols, moved_bytes=8 * rows * cols)
    head, d_head, shares = call(
        lambda *refs: second_edge(tiles, rows, *refs), "second_edge", [VMEM] * 7,
        (arr(PACK, cols), arr(PACK, cols, dtype=BF16), arr(1, 128)), [VMEM] * 3,
        (down, halo, l_head, lev[:PACK], sums, b[:PACK], r[:PACK]), flops=cols, moved_bytes=cols)

    stages = exchange_stages(tiles)
    done = 0
    met = partner(shares, stages[done])
    edge_scratch = [pltpu.VMEM((PACK, cols), BF16)]
    held, drags = call(
        lambda *refs: start_blocks((2, 3), *refs), "start_sent", [SMEM] + [VMEM] * 6,
        (arr(4, side, side, dtype=BF16), arr(2, side, side, dtype=BF16)), [VMEM] * 2,
        (plan, x, y, d, d_head, sm, sm_t), edge_scratch, flops=dots(4, EARLY), moved_bytes=rows * cols)

    def next_stage(shares, met, done, *after):
        shares = shares + met
        done += 1
        shares, *after = lax.optimization_barrier((shares,) + after)
        return shares, partner(shares, stages[done]), done, tuple(after)

    shares, met, done, (held,) = next_stage(shares, met, done, held)
    pair = arr(2, side, side, dtype=BF16)
    sent, near, far = call(
        finish_sent, "finish_sent", [VMEM] * 4, (arr(2, 2, side, side), pair, pair), [VMEM] * 3,
        (sm, sm_t, held, drags), [squares(4)], flops=dots(4, SUB - EARLY), moved_bytes=rows * cols)
    far = moved(far, 2)
    near = moved(near, 1)
    if done < len(stages) - 1:
        shares, met, done, (sent,) = next_stage(shares, met, done, sent)
    held, drags = call(
        lambda *refs: start_blocks((1,), *refs), "start_own", [SMEM] + [VMEM] * 6,
        (arr(2, side, side, dtype=BF16), arr(1, side, side, dtype=BF16)), [VMEM] * 2,
        (plan, x, y, d, d_head, sm, sm_t), edge_scratch, flops=dots(2, EARLY), moved_bytes=rows * cols)
    if done < len(stages) - 1:
        shares, met, done, (held,) = next_stage(shares, met, done, held)
    copies = 2 + 3 * (plan.shape[1] + 1)
    x, y, level, resident = call(
        finish_own, "finish_own", [SMEM] + [VMEM] * 9, (field, field, field, arr(3, 2, side, side)), [HBM] * 4,
        (plan, sm, sm_t, held, drags, x, y, lev, head, sent),
        [squares(2), pltpu.VMEM((2, side, side), F32), pltpu.SemaphoreType.DMA((copies,))],
        flops=dots(2, SUB - EARLY), moved_bytes=12 * rows * cols)
    if done < len(stages) - 1:
        shares, met, done, (resident,) = next_stage(shares, met, done, resident)
    while done < len(stages) - 1:
        shares, met, done, _ = next_stage(shares, met, done)
    resident = call(
        settle_resident, "settle_resident", [VMEM, VMEM, HBM], arr(3, 2, side, side), HBM,
        (near, far, resident),
        [pltpu.VMEM((2, 2, side, side), F32), pltpu.SemaphoreType.DMA((2,))],
        aliases={2: 0}, moved_bytes=24 * side * side)
    energy = call(add_shares, "add_shares", [VMEM] * 2, arr(2), SMEM, (shares, met))
    return level, x, y, resident, energy


def solution(mesh):
    cut = P(("ens", "tile"), None)
    return jax.shard_map(
        on_device,
        mesh=mesh,
        in_specs=(cut,) * 6 + (P(), cut),
        out_specs=(cut, cut, cut, P(("ens", "tile"), None, None, None), P("ens")),
        check_vma=False,
    )
```

```python
import jax
import jax.numpy as jnp
from jax import lax
from jax.experimental import pallas as pl
from jax.experimental.pallas import tpu as pltpu
from jax.sharding import PartitionSpec as P

SUB = 12
PIECES = (6, 6)
EDGE = 8
PACK = 16
BAND = 32
LOAD = 64
GRANT = 16 * 2**20
F32 = jnp.float32
BF16 = jnp.bfloat16
VMEM = pl.BlockSpec(memory_space=pltpu.VMEM)
SMEM = pl.BlockSpec(memory_space=pltpu.SMEM)
HBM = pl.BlockSpec(memory_space=pltpu.HBM)


def shifted_left(rows, half):
    cols = rows.shape[1]
    ids = lax.broadcasted_iota(jnp.int32, rows.shape, 1) % half
    return jnp.where(ids == half - 1, 0.0, pltpu.roll(rows, cols - 1, 1))


def shifted_right(rows, half):
    ids = lax.broadcasted_iota(jnp.int32, rows.shape, 1) % half
    return jnp.where(ids == 0, 0.0, pltpu.roll(rows, 1, 1))


def drag_of(rough, level, depth):
    return (rough / jnp.maximum(level + depth, 1.0)).astype(BF16)


def code_column(plan, code, side):
    column = 0
    for k in range(plan.shape[1]):
        column = column + jnp.where(plan[0, k] == code, k * side, 0)
    return pl.multiple_of(column, side)


def of_code(code, codes, rows, side):
    block = jnp.zeros((rows.shape[0], side), rows.dtype)
    for k in range(codes.shape[1]):
        block = jnp.where(codes[0:1, k:k + 1] == code, rows[:, k * side:(k + 1) * side], block)
    return block


def put_blocks(plan, x, y, drag, held, drags):
    side = held.shape[-1]
    for k in range(plan.shape[1]):
        code, span = plan[0, k], pl.ds(k * side, side)
        held[code, 0] = x[:, span].astype(BF16)
        held[code, 1] = y[:, span].astype(BF16)
        drags[code] = drag[:, span]


def advance(half, level, ahead, flow_x, flow_y, celerity, above_x):
    rows = level.shape[0]
    row_ids = lax.broadcasted_iota(jnp.int32, level.shape, 0)
    below = jnp.where(row_ids == rows - 1, ahead, pltpu.roll(level, rows - 1, 0))
    new_x = flow_x - celerity * (below - level)
    new_y = flow_y - celerity * (shifted_left(level, half) - level)
    behind_x = jnp.where(row_ids == 0, above_x, pltpu.roll(new_x, 1, 0))
    new_level = level - (new_x - behind_x) - (new_y - shifted_right(new_y, half))
    return new_x, new_y, new_level


def edge_rows(s, x, y, c, up, down, first, heads, tails, sems):
    rows = s.shape[0]
    copies = []
    for j, array in enumerate((s, x, y, c)):
        copies.append(pltpu.make_async_copy(array.at[pl.ds(0, EDGE)], heads.at[j], sems.at[2 * j]))
        copies.append(pltpu.make_async_copy(array.at[pl.ds(rows - EDGE, EDGE)], tails.at[j], sems.at[2 * j + 1]))
    for copy in copies:
        copy.start()
    for copy in copies:
        copy.wait()
    up[0:2] = heads[0, 0:2]
    for j in range(1, 4):
        up[j + 1:j + 2] = heads[j, 0:1]
    down[0:2] = tails[0, EDGE - 2:]
    down[2:4] = tails[1, EDGE - 2:]
    down[4:6] = tails[3, EDGE - 2:]
    down[6:7] = tails[2, EDGE - 1:]
    first[...] = heads[0, 0:1]


def first_step(s_in, x_in, y_in, c, b, r, sm, x_out, y_out, l_out, d_out, sm_t, s, x, y, sems):
    total, cols = s.shape
    half = cols // 2
    loads = total // LOAD
    pairs = ((s_in, s), (x_in, x), (y_in, y))

    def copy(i, j):
        rows = pl.ds(i * LOAD, LOAD)
        source, target = pairs[j]
        return pltpu.make_async_copy(source.at[rows], target.at[rows], sems.at[i, j])

    for i in range(loads):
        for j in range(len(pairs)):
            copy(i, j).start()
    sm_t[...] = sm[...].T
    above = jnp.zeros((1, cols), F32)
    for j in range(len(pairs)):
        copy(0, j).wait()
    for i in range(loads):
        if i + 1 < loads:
            for j in range(len(pairs)):
                copy(i + 1, j).wait()
        for start in range(i * LOAD, (i + 1) * LOAD, BAND):
            rows = pl.ds(start, BAND)
            if start + BAND < total:
                ahead = s[pl.ds(start + BAND, 1)]
            else:
                ahead = jnp.zeros((1, cols), F32)
            new_x, new_y, level = advance(half, s[rows], ahead, x[rows], y[rows], c[rows], above)
            above = new_x[BAND - 1:]
            x_out[rows] = new_x
            y_out[rows] = new_y
            l_out[rows] = level
            d_out[rows] = drag_of(r[rows], level, b[rows])


def row_weight(shape, start, total_rows):
    ids = lax.broadcasted_iota(jnp.int32, shape, 0) + start
    return 1.0 + ids.astype(F32) * (2.0 / total_rows)


def second_step(tile_count, plan_in, l_in, l_head, l_tail, halo, x_in, y_in, c, b, r,
                x_out, y_out, l_out, held, drags, sums_out, plan, drag, plan_sem):
    total, cols = l_in.shape
    half = cols // 2
    bands = total // BAND
    position = lax.axis_index("tile")
    plan_copy = pltpu.make_async_copy(plan_in, plan, plan_sem)
    plan_copy.start()

    def level_band(i):
        start, stop = i * BAND, (i + 1) * BAND
        parts = [l_in[pl.ds(start, BAND)]]
        if i == 0:
            parts = [l_head[...], l_in[pl.ds(EDGE, BAND - EDGE)]]
        if i == bands - 1:
            parts = [l_in[pl.ds(start, BAND - EDGE)], l_tail[...]]
        return jnp.concatenate(parts, 0)

    above = jnp.zeros((1, cols), F32)
    sums = jnp.zeros((EDGE, cols), F32)
    level = level_band(0)
    for i in range(bands):
        rows = pl.ds(i * BAND, BAND)
        following = level_band(i + 1) if i + 1 < bands else halo[...]
        new_x, new_y, new_level = advance(half, level, following[0:1], x_in[rows], y_in[rows], c[rows], above)
        level = following
        above = new_x[BAND - 1:]
        x_out[rows] = new_x
        y_out[rows] = new_y
        l_out[rows] = new_level
        drag[rows] = drag_of(r[rows], new_level, b[rows])
        for j in range(BAND // EDGE):
            if i + j > 0:
                part = new_level[j * EDGE:(j + 1) * EDGE]
                weight = row_weight(part.shape, position * total + i * BAND + j * EDGE, tile_count * total)
                sums = sums + weight * (part * part)
    sums_out[...] = sums
    plan_copy.wait()
    put_blocks(plan, x_out, y_out, drag, held, drags)


def second_edge(tile_count, row_count, plan, down, halo, l_head, l2_head, sums, b_head, r_head, drags_in, head, drags, shares):
    cols = l_head.shape[1]
    half = cols // 2
    position = lax.axis_index("tile")
    total_rows = tile_count * row_count
    has_previous = jnp.where(position == 0, 0.0, 1.0)
    above_x = has_previous * (down[...] - halo[2:3] * (l_head[0:1] - halo[1:2]))
    row_ids = lax.broadcasted_iota(jnp.int32, (PACK, cols), 0)
    level = l2_head[...] + jnp.where(row_ids == 0, above_x, 0.0)
    head[...] = level
    drag, codes = drag_of(r_head[...], level, b_head[...]).astype(F32), plan[...]
    for slot in range(drags.shape[0]):
        drags[slot] = drags_in[slot + 1]
        drags[slot, 0:PACK] = of_code(slot + 1, codes, drag, drags.shape[-1]).astype(BF16)
    top = level[:EDGE]
    whole = sums[...] + row_weight(top.shape, position * row_count, total_rows) * (top * top)
    lanes = lax.broadcasted_iota(jnp.int32, (1, 128), 1)
    share = jnp.zeros((1, 128), F32)
    for scenario in range(2):
        part = whole[:, scenario * half:(scenario + 1) * half]
        share = jnp.where(lanes == 2 * position + scenario, jnp.sum(part) * (1.0 / (total_rows * half)), share)
    shares[...] = share


def soften(smooth, smooth_t, source, held, drags, repeats, put=None):
    for repeat in range(repeats):
        for slot in range(drags.shape[0]):
            for f in range(2):
                start = source if repeat == 0 else held
                mixed = jnp.dot(start[slot, f], smooth_t, preferred_element_type=F32).astype(BF16)
                full = jnp.dot(smooth, mixed, preferred_element_type=F32)
                settled = full / (1.0 + drags[slot].astype(F32) * jnp.abs(full))
                if put is None or repeat + 1 < repeats:
                    held[slot, f] = settled.astype(BF16)
                else:
                    put(slot, f, settled)


def smooth_all(tile_count, plan_in, up, down, first, c, b, r, sm, sm_t, x_in, y_in, l_in, d_in,
               x, y, l_head, l_tail, halo, x_last, held, drags, edge, low_x, plan, plan_sem):
    plan_copy = pltpu.make_async_copy(plan_in, plan, plan_sem)
    plan_copy.start()
    rows, cols = x.shape
    half = cols // 2
    side = sm.shape[0]
    position = lax.axis_index("tile")
    has_next = jnp.where(position == tile_count - 1, 0.0, 1.0)
    has_previous = jnp.where(position == 0, 0.0, 1.0)
    below = up[...] * has_next
    above = down[...] * has_previous
    tail, head = pl.ds(rows - EDGE, EDGE), pl.ds(0, EDGE)
    row_ids = lax.broadcasted_iota(jnp.int32, (EDGE, cols), 0)
    own_first = first[...]

    change = jnp.where(row_ids == EDGE - 1, c[tail] * below[0:1], 0.0)
    x_tail = x_in[tail] - change
    low_x[0:EDGE] = x_in[pl.ds(rows - PACK, EDGE)]
    low_x[EDGE:PACK] = x_tail
    low = l_in[tail] + change
    l_tail[...] = low
    above_x = above[3:4] - above[5:6] * (own_first - above[1:2])
    top = l_in[head] + jnp.where(row_ids == 0, above_x, 0.0)
    l_head[...] = top

    next_x = below[2:3] - below[4:5] * (below[1:2] - below[0:1])
    next_y = below[3:4] - below[4:5] * (shifted_left(below[0:1], half) - below[0:1])
    next_level = below[0:1] - (next_x - x_tail[EDGE - 1:]) - (next_y - shifted_right(next_y, half))
    halo[0:1] = has_next * next_level
    before_x = above[2:3] - above[4:5] * (above[1:2] - above[0:1])
    before_y = above[6:7] - above[5:6] * (shifted_left(above[1:2], half) - above[1:2])
    halo[1:2] = above[1:2] - (above_x - before_x) - (before_y - shifted_right(before_y, half))
    halo[2:3] = above[5:6]

    first_rows, last_rows = pl.ds(0, PACK), pl.ds(rows - PACK, PACK)
    first_edge, last_edge = pl.ds(0, PACK), pl.ds(PACK, PACK)
    edge[first_edge] = drag_of(r[first_rows], jnp.concatenate([top, l_in[pl.ds(EDGE, EDGE)]], 0), b[first_rows])
    edge[last_edge] = drag_of(r[last_rows], jnp.concatenate([l_in[pl.ds(rows - PACK, EDGE)], low], 0), b[last_rows])
    plan_copy.wait()
    dry = pl.ds(code_column(plan, 0, side), side)
    x[:, dry] = x_in[:, dry]
    x[last_rows, dry] = low_x[:, dry]
    y[:, dry] = y_in[:, dry]
    columns = [code_column(plan, code, side) for code in (1, 2, 3)]
    for slot, column in enumerate(columns):
        span = pl.ds(column, side)
        drags[slot] = d_in[:, span]
        drags[slot, first_rows] = edge[first_edge, span]
        drags[slot, last_rows] = edge[last_edge, span]
        held[slot, 0] = x_in[:, span].astype(BF16)
        held[slot, 0, last_rows] = low_x[:, span].astype(BF16)
        held[slot, 1] = y_in[:, span].astype(BF16)

    def put(slot, f, settled):
        (x, y)[f][:, pl.ds(columns[slot], side)] = settled

    soften(sm[...], sm_t[...], held, held, drags, SUB, put)
    x_last[...] = x[rows - 1:rows]


def start_last(repeats, sm, sm_t, held_in, drags, l_in, head, held, lev, sems):
    rest, top = pl.ds(PACK, l_in.shape[0] - PACK), pl.ds(0, PACK)
    copies = [
        pltpu.make_async_copy(l_in.at[rest], lev.at[rest], sems.at[0]),
        pltpu.make_async_copy(head.at[top], lev.at[top], sems.at[1]),
    ]
    for copy in copies:
        copy.start()
    soften(sm[...], sm_t[...], held_in.at[pl.ds(1, 3)], held, drags, repeats)
    for copy in copies:
        copy.wait()


def go_on(repeats, sm, sm_t, held_in, drags, held):
    soften(sm[...], sm_t[...], held_in, held, drags, repeats)


def finish_last(repeats, plan_in, sm, sm_t, held_in, drags, x_in, y_in, x, y, own, near, far, held, plan, plan_sem):
    plan_copy = pltpu.make_async_copy(plan_in, plan, plan_sem)
    plan_copy.start()
    side = sm.shape[0]
    columns = []

    def put(slot, f, settled):
        if not columns:
            plan_copy.wait()
            columns.extend(code_column(plan, code, side) for code in range(4))
        (x, y)[f][:, pl.ds(columns[slot + 1], side)] = settled
        if slot == 0:
            own[f] = settled
        else:
            (near, far)[slot - 1][f] = settled.astype(BF16)

    soften(sm[...], sm_t[...], held_in, held, drags, repeats, put)
    dry = pl.ds(columns[0], side)
    x[:, dry] = x_in[:, dry]
    y[:, dry] = y_in[:, dry]


def put_fluxes(x_in, y_in, own, x, y, resident, sems):
    copies = [
        pltpu.make_async_copy(source, target, sems.at[i])
        for i, (source, target) in enumerate(((x_in, x), (y_in, y), (own, resident.at[0])))
    ]
    for copy in copies:
        copy.start()
    for copy in copies:
        copy.wait()


def put_received(near, far, resident_held, resident, stage, sems):
    copies = []
    for slot, block in enumerate((near, far)):
        stage[slot] = block[...].astype(F32)
        copies.append(pltpu.make_async_copy(stage.at[slot], resident.at[slot + 1], sems.at[slot]))
        copies[-1].start()
    for copy in copies:
        copy.wait()


def add_shares(mine, received, energy):
    shares = mine[...] + received[...]
    lanes = lax.broadcasted_iota(jnp.int32, shares.shape, 1)
    for scenario in range(2):
        energy[scenario] = jnp.sum(jnp.where(lanes % 2 == scenario, shares, 0.0))


def moved(value, steps):
    count = lax.axis_size("tile")
    return lax.ppermute(value, "tile", [(i, (i + steps) % count) for i in range(count)])


def exchange_stages(count):
    deep = 8 if count >= 16 else max(count // 2, 1)
    wide = count // (2 * deep)

    def index(x, z, core):
        return (x * deep + z) * 2 + core

    def stage(rule):
        pairs = []
        for i in range(count):
            core, z, x = i % 2, (i // 2) % deep, i // (2 * deep)
            pairs.append((i, index(*rule(x, z, core))))
        return pairs

    stages = []
    if deep == 8:
        across = {0: 6, 6: 0, 2: 4, 4: 2, 1: 7, 7: 1, 3: 5, 5: 3}
        stages.append(stage(lambda x, z, core: (x, z ^ 2, core)))
        stages.append(stage(lambda x, z, core: (x, across[z], core)))
    if wide >= 2:
        stages.append(stage(lambda x, z, core: (x ^ 1, z, core)))
    if wide == 4:
        stages.append(stage(lambda x, z, core: (3 - x, z, core)))
    stages.append(stage(lambda x, z, core: (x, z, 1 - core)))
    reach = 1
    while reach < (2 if deep == 8 else deep):
        stages.append(stage(lambda x, z, core, reach=reach: (x, z ^ reach, core)))
        reach *= 2
    return stages


def on_device(surface, flux_x, flux_y, celerity, bed_depth, roughness, smoother, plan):
    rows, cols = surface.shape
    side = smoother.shape[0]
    tiles = lax.axis_size("tile")

    def arr(*shape, dtype=F32):
        return jax.ShapeDtypeStruct(shape, dtype)

    field, square = arr(rows, cols), arr(side, side, dtype=BF16)

    def call(body, name, ins, outs, out_specs, operands, scratch=(), aliases={}, flops=0, moved_bytes=0):
        return pl.pallas_call(
            body,
            out_shape=outs,
            in_specs=ins,
            out_specs=out_specs,
            scratch_shapes=scratch,
            input_output_aliases=aliases,
            compiler_params=pltpu.CompilerParams(vmem_limit_bytes=GRANT),
            cost_estimate=pl.CostEstimate(flops=flops, bytes_accessed=moved_bytes, transcendentals=0),
            name=name,
        )(*operands)

    def dots(chains, repeats):
        return chains * repeats * 4 * side**3

    def partner(value, pairs):
        return lax.ppermute(value, "tile", pairs)

    c, b, r, sm = celerity, bed_depth, roughness, smoother
    codes = plan
    surface, flux_x, flux_y, celerity, plan = [
        pltpu.with_memory_space_constraint(array, pltpu.HBM)
        for array in (surface, flux_x, flux_y, celerity, plan)
    ]
    plan_scratch = [pltpu.SMEM(plan.shape, plan.dtype), pltpu.SemaphoreType.DMA]
    held_shape, drag_shape = arr(4, 2, side, side, dtype=BF16), arr(4, side, side, dtype=BF16)
    wet_held, wet_drags = arr(3, 2, side, side, dtype=BF16), arr(3, side, side, dtype=BF16)
    up, down, first = call(
        edge_rows, "edge_rows", [HBM] * 4, (arr(5, cols), arr(7, cols), arr(1, cols)), [VMEM] * 3,
        (surface, flux_x, flux_y, celerity),
        [pltpu.VMEM((4, EDGE, cols), F32)] * 2 + [pltpu.SemaphoreType.DMA((8,))])
    up = moved(up, -1)
    down = moved(down, 1)
    x, y, lev, d, sm_t = call(
        first_step, "first_step", [HBM] * 3 + [VMEM] * 4,
        (field, field, field, arr(rows, cols, dtype=BF16), square), [VMEM] * 5,
        (surface, flux_x, flux_y, c, b, r, sm),
        [pltpu.VMEM((rows, cols), F32)] * 3 + [pltpu.SemaphoreType.DMA((rows // LOAD, 3))],
        flops=20 * rows * cols, moved_bytes=24 * rows * cols)
    held_scratch, drag_scratch = pltpu.VMEM(wet_held.shape, BF16), pltpu.VMEM(wet_drags.shape, BF16)
    x, y, l_head, l_tail, halo, x_last = call(
        lambda *refs: smooth_all(tiles, *refs), "smooth_all", [HBM] + [VMEM] * 12,
        (field, field, arr(EDGE, cols), arr(EDGE, cols), arr(3, cols), arr(1, cols)), [VMEM] * 6,
        (plan, up, down, first, c, b, r, sm, sm_t, x, y, lev, d),
        [held_scratch, drag_scratch, pltpu.VMEM((2 * PACK, cols), BF16), pltpu.VMEM((PACK, cols), F32)] + plan_scratch,
        flops=dots(6, SUB), moved_bytes=8 * rows * cols)
    down = moved(x_last, 1)
    x, y, lev, held, drags, sums = call(
        lambda *refs: second_step(tiles, *refs), "second_step", [HBM] + [VMEM] * 9,
        (field, field, field, held_shape, drag_shape, arr(EDGE, cols)), [VMEM] * 6,
        (plan, lev, l_head, l_tail, halo, x, y, c, b, r),
        plan_scratch[:1] + [pltpu.VMEM((rows, cols), BF16)] + plan_scratch[1:],
        flops=20 * rows * cols, moved_bytes=8 * rows * cols)
    head, drags, shares = call(
        lambda *refs: second_edge(tiles, rows, *refs), "second_edge", [VMEM] * 9,
        (arr(PACK, cols), wet_drags, arr(1, 128)), [VMEM] * 3,
        (codes, down, halo, l_head, lev[:PACK], sums, b[:PACK], r[:PACK], drags), flops=cols, moved_bytes=cols)

    stages = exchange_stages(tiles)
    done = 0

    def exchange(shares, beside):
        nonlocal done
        if done + 1 >= len(stages):
            return (shares,) + tuple(beside())
        met = lax.ppermute(shares, "tile", stages[done])
        done += 1
        return lax.optimization_barrier((shares + met,) + tuple(beside()))

    pair, resident_shape = arr(2, side, side, dtype=BF16), arr(3, 2, side, side)
    shares, held, level = exchange(shares, lambda: call(
        lambda *refs: start_last(PIECES[0], *refs), "start_last", [VMEM] * 6, (wet_held, field), [VMEM, HBM],
        (sm, sm_t, held, drags, lev, head), [pltpu.SemaphoreType.DMA((2,))],
        flops=dots(6, PIECES[0]), moved_bytes=rows * cols))
    for piece in PIECES[1:-1]:
        shares, held = exchange(shares, lambda: (call(
            lambda *refs: go_on(piece, *refs), "go_on", [VMEM] * 4, wet_held, VMEM, (sm, sm_t, held, drags),
            flops=dots(6, piece), moved_bytes=rows * cols),))
    shares, x, y, own, near, far = exchange(shares, lambda: call(
        lambda *refs: finish_last(PIECES[-1], *refs), "finish_last", [HBM] + [VMEM] * 6,
        (field, field, arr(2, side, side), pair, pair), [VMEM] * 5,
        (plan, sm, sm_t, held, drags, x, y), [held_scratch] + plan_scratch,
        flops=dots(6, PIECES[-1]), moved_bytes=rows * cols))
    near, far = moved(near, 1), moved(far, 2)
    shares, x, y, resident = exchange(shares, lambda: call(
        put_fluxes, "put_fluxes", [VMEM] * 3, (field, field, resident_shape), [HBM] * 3,
        (x, y, own), [pltpu.SemaphoreType.DMA((3,))], moved_bytes=16 * rows * cols))
    while done + 1 < len(stages):
        shares, = exchange(shares, tuple)
    met = lax.ppermute(shares, "tile", stages[done])
    resident = call(
        put_received, "put_received", [VMEM] * 2 + [HBM], resident_shape, HBM, (near, far, resident),
        [pltpu.VMEM((2, 2, side, side), F32), pltpu.SemaphoreType.DMA((2,))],
        aliases={2: 0}, moved_bytes=24 * side * side)
    energy = call(add_shares, "add_shares", [VMEM] * 2, arr(2), SMEM, (shares, met))
    return level, x, y, resident, energy


def solution(mesh):
    cut = P(("ens", "tile"), None)
    return jax.shard_map(
        on_device,
        mesh=mesh,
        in_specs=(cut,) * 6 + (P(), cut),
        out_specs=(cut, cut, cut, P(("ens", "tile"), None, None, None), P("ens")),
        check_vma=False,
    )
```

```python
import jax
import jax.numpy as jnp
from jax import lax
from jax.experimental import pallas as pl
from jax.experimental.pallas import tpu as pltpu
from jax.sharding import PartitionSpec as P

SUB = 12
HALF = 6
EDGE = 8
PACK = 16
BAND = 32
LOAD = 64
GRANT = 16 * 2**20
F32 = jnp.float32
BF16 = jnp.bfloat16
VMEM = pl.BlockSpec(memory_space=pltpu.VMEM)
SMEM = pl.BlockSpec(memory_space=pltpu.SMEM)
HBM = pl.BlockSpec(memory_space=pltpu.HBM)


def shifted_left(rows, half):
    cols = rows.shape[1]
    ids = lax.broadcasted_iota(jnp.int32, rows.shape, 1) % half
    return jnp.where(ids == half - 1, 0.0, pltpu.roll(rows, cols - 1, 1))


def shifted_right(rows, half):
    ids = lax.broadcasted_iota(jnp.int32, rows.shape, 1) % half
    return jnp.where(ids == 0, 0.0, pltpu.roll(rows, 1, 1))


def drag_of(rough, level, depth):
    return (rough / jnp.maximum(level + depth, 1.0)).astype(BF16)


def code_column(codes, code, side):
    place = lax.broadcasted_iota(jnp.int32, codes.shape, 1) * side
    column = jnp.sum(jnp.where(codes == code, place, 0).astype(F32))
    return pl.multiple_of(column.astype(jnp.int32), side)


def advance(half, level, ahead, flow_x, flow_y, celerity, above_x):
    rows = level.shape[0]
    row_ids = lax.broadcasted_iota(jnp.int32, level.shape, 0)
    below = jnp.where(row_ids == rows - 1, ahead, pltpu.roll(level, rows - 1, 0))
    new_x = flow_x - celerity * (below - level)
    new_y = flow_y - celerity * (shifted_left(level, half) - level)
    behind_x = jnp.where(row_ids == 0, above_x, pltpu.roll(new_x, 1, 0))
    new_level = level - (new_x - behind_x) - (new_y - shifted_right(new_y, half))
    return new_x, new_y, new_level


def edge_rows(s, x, y, c, up, down, first, heads, tails, sems):
    rows = s.shape[0]
    copies = []
    for j, array in enumerate((s, x, y, c)):
        copies.append(pltpu.make_async_copy(array.at[pl.ds(0, EDGE)], heads.at[j], sems.at[2 * j]))
        copies.append(pltpu.make_async_copy(array.at[pl.ds(rows - EDGE, EDGE)], tails.at[j], sems.at[2 * j + 1]))
    for copy in copies:
        copy.start()
    for copy in copies:
        copy.wait()
    up[0:2] = heads[0, 0:2]
    for j in range(1, 4):
        up[j + 1:j + 2] = heads[j, 0:1]
    down[0:2] = tails[0, EDGE - 2:]
    down[2:4] = tails[1, EDGE - 2:]
    down[4:6] = tails[3, EDGE - 2:]
    down[6:7] = tails[2, EDGE - 1:]
    first[...] = heads[0, 0:1]


def first_step(s_in, x_in, y_in, c, b, r, sm, x_out, y_out, l_out, d_out, sm_t, s, x, y, sems):
    total, cols = s.shape
    half = cols // 2
    loads = total // LOAD
    pairs = ((s_in, s), (x_in, x), (y_in, y))

    def copy(i, j):
        rows = pl.ds(i * LOAD, LOAD)
        source, target = pairs[j]
        return pltpu.make_async_copy(source.at[rows], target.at[rows], sems.at[i, j])

    for i in range(loads):
        for j in range(len(pairs)):
            copy(i, j).start()
    sm_t[...] = sm[...].T
    above = jnp.zeros((1, cols), F32)
    for j in range(len(pairs)):
        copy(0, j).wait()
    for i in range(loads):
        if i + 1 < loads:
            for j in range(len(pairs)):
                copy(i + 1, j).wait()
        for start in range(i * LOAD, (i + 1) * LOAD, BAND):
            rows = pl.ds(start, BAND)
            if start + BAND < total:
                ahead = s[pl.ds(start + BAND, 1)]
            else:
                ahead = jnp.zeros((1, cols), F32)
            new_x, new_y, level = advance(half, s[rows], ahead, x[rows], y[rows], c[rows], above)
            above = new_x[BAND - 1:]
            x_out[rows] = new_x
            y_out[rows] = new_y
            l_out[rows] = level
            d_out[rows] = drag_of(r[rows], level, b[rows])


def row_weight(shape, start, total_rows):
    ids = lax.broadcasted_iota(jnp.int32, shape, 0) + start
    return 1.0 + ids.astype(F32) * (2.0 / total_rows)


def second_step(tile_count, l_in, l_head, l_tail, halo, x_in, y_in, c, b, r, x_out, y_out, l_out, d_out, sums_out):
    total, cols = l_in.shape
    half = cols // 2
    bands = total // BAND
    position = lax.axis_index("tile")

    def level_band(i):
        start, stop = i * BAND, (i + 1) * BAND
        parts = [l_in[pl.ds(start, BAND)]]
        if i == 0:
            parts = [l_head[...], l_in[pl.ds(EDGE, BAND - EDGE)]]
        if i == bands - 1:
            parts = [l_in[pl.ds(start, BAND - EDGE)], l_tail[...]]
        return jnp.concatenate(parts, 0)

    above = jnp.zeros((1, cols), F32)
    sums = jnp.zeros((EDGE, cols), F32)
    level = level_band(0)
    for i in range(bands):
        rows = pl.ds(i * BAND, BAND)
        following = level_band(i + 1) if i + 1 < bands else halo[...]
        new_x, new_y, new_level = advance(half, level, following[0:1], x_in[rows], y_in[rows], c[rows], above)
        level = following
        above = new_x[BAND - 1:]
        x_out[rows] = new_x
        y_out[rows] = new_y
        l_out[rows] = new_level
        d_out[rows] = drag_of(r[rows], new_level, b[rows])
        for j in range(BAND // EDGE):
            if i + j > 0:
                part = new_level[j * EDGE:(j + 1) * EDGE]
                weight = row_weight(part.shape, position * total + i * BAND + j * EDGE, tile_count * total)
                sums = sums + weight * (part * part)
    sums_out[...] = sums


def second_edge(tile_count, row_count, down, halo, l_head, l2_head, sums, b_head, r_head, head, d_head, shares):
    cols = l_head.shape[1]
    half = cols // 2
    position = lax.axis_index("tile")
    total_rows = tile_count * row_count
    has_previous = jnp.where(position == 0, 0.0, 1.0)
    above_x = has_previous * (down[...] - halo[2:3] * (l_head[0:1] - halo[1:2]))
    row_ids = lax.broadcasted_iota(jnp.int32, (PACK, cols), 0)
    level = l2_head[...] + jnp.where(row_ids == 0, above_x, 0.0)
    head[...] = level
    d_head[...] = drag_of(r_head[...], level, b_head[...])
    top = level[:EDGE]
    whole = sums[...] + row_weight(top.shape, position * row_count, total_rows) * (top * top)
    lanes = lax.broadcasted_iota(jnp.int32, (1, 128), 1)
    share = jnp.zeros((1, 128), F32)
    for scenario in range(2):
        part = whole[:, scenario * half:(scenario + 1) * half]
        share = jnp.where(lanes == 2 * position + scenario, jnp.sum(part) * (1.0 / (total_rows * half)), share)
    shares[...] = share


def soften(smooth, smooth_t, source, held, drags, repeats, put=None):
    for repeat in range(repeats):
        for slot in range(drags.shape[0]):
            for f in range(2):
                block = source(slot, f) if repeat == 0 else held[slot, f]
                mixed = jnp.dot(block, smooth_t, preferred_element_type=F32).astype(BF16)
                full = jnp.dot(smooth, mixed, preferred_element_type=F32)
                settled = full / (1.0 + drags[slot].astype(F32) * jnp.abs(full))
                if put is None or repeat + 1 < repeats:
                    held[slot, f] = settled.astype(BF16)
                else:
                    put(slot, f, settled)


def smooth_all(tile_count, plan, up, down, first, c, b, r, sm, sm_t, x_in, y_in, l_in, d_in,
               x, y, l_head, l_tail, halo, x_last, held, drags, edge, low_x):
    rows, cols = x.shape
    half = cols // 2
    side = sm.shape[0]
    position = lax.axis_index("tile")
    has_next = jnp.where(position == tile_count - 1, 0.0, 1.0)
    has_previous = jnp.where(position == 0, 0.0, 1.0)
    below = up[...] * has_next
    above = down[...] * has_previous
    tail, head = pl.ds(rows - EDGE, EDGE), pl.ds(0, EDGE)
    row_ids = lax.broadcasted_iota(jnp.int32, (EDGE, cols), 0)
    own_first = first[...]

    change = jnp.where(row_ids == EDGE - 1, c[tail] * below[0:1], 0.0)
    x_tail = x_in[tail] - change
    low_x[0:EDGE] = x_in[pl.ds(rows - PACK, EDGE)]
    low_x[EDGE:PACK] = x_tail
    low = l_in[tail] + change
    l_tail[...] = low
    above_x = above[3:4] - above[5:6] * (own_first - above[1:2])
    top = l_in[head] + jnp.where(row_ids == 0, above_x, 0.0)
    l_head[...] = top

    next_x = below[2:3] - below[4:5] * (below[1:2] - below[0:1])
    next_y = below[3:4] - below[4:5] * (shifted_left(below[0:1], half) - below[0:1])
    next_level = below[0:1] - (next_x - x_tail[EDGE - 1:]) - (next_y - shifted_right(next_y, half))
    halo[0:1] = has_next * next_level
    before_x = above[2:3] - above[4:5] * (above[1:2] - above[0:1])
    before_y = above[6:7] - above[5:6] * (shifted_left(above[1:2], half) - above[1:2])
    halo[1:2] = above[1:2] - (above_x - before_x) - (before_y - shifted_right(before_y, half))
    halo[2:3] = above[5:6]

    first_rows, last_rows = pl.ds(0, PACK), pl.ds(rows - PACK, PACK)
    first_edge, last_edge = pl.ds(0, PACK), pl.ds(PACK, PACK)
    edge[first_edge] = drag_of(r[first_rows], jnp.concatenate([top, l_in[pl.ds(EDGE, EDGE)]], 0), b[first_rows])
    edge[last_edge] = drag_of(r[last_rows], jnp.concatenate([l_in[pl.ds(rows - PACK, EDGE)], low], 0), b[last_rows])
    codes = plan[...]
    dry = pl.ds(code_column(codes, 0, side), side)
    x[:, dry] = x_in[:, dry]
    x[last_rows, dry] = low_x[:, dry]
    y[:, dry] = y_in[:, dry]
    columns = [code_column(codes, code, side) for code in (1, 2, 3)]
    for slot, column in enumerate(columns):
        span = pl.ds(column, side)
        drags[slot] = d_in[:, span]
        drags[slot, first_rows] = edge[first_edge, span]
        drags[slot, last_rows] = edge[last_edge, span]
        held[slot, 0] = x_in[:, span].astype(BF16)
        held[slot, 0, last_rows] = low_x[:, span].astype(BF16)
        held[slot, 1] = y_in[:, span].astype(BF16)

    def put(slot, f, settled):
        (x, y)[f][:, pl.ds(columns[slot], side)] = settled

    soften(sm[...], sm_t[...], lambda slot, f: held[slot, f], held, drags, SUB, put)
    x_last[...] = x[rows - 1:rows]


def start_last(repeats, plan, sm, sm_t, x, y, d, d_head, held, drags, edge):
    side = sm.shape[0]
    codes = plan[...]
    edge[...] = d_head[...]
    spans = [pl.ds(code_column(codes, code, side), side) for code in (1, 2, 3)]
    for slot, span in enumerate(spans):
        drags[slot] = d[:, span]
        drags[slot, 0:PACK] = edge[:, span]
    soften(sm[...], sm_t[...], lambda slot, f: (x, y)[f][:, spans[slot]].astype(BF16), held, drags, repeats)


def finish_last(repeats, plan, sm, sm_t, held_in, drags, x_in, y_in, x, y, own, near, far, held):
    side = sm.shape[0]
    codes = plan[...]
    dry, *spans = [pl.ds(code_column(codes, code, side), side) for code in range(4)]

    def put(slot, f, settled):
        (x, y)[f][:, spans[slot]] = settled
        if slot == 0:
            own[f] = settled
        else:
            (near, far)[slot - 1][f] = settled.astype(BF16)

    soften(sm[...], sm_t[...], lambda slot, f: held_in[slot, f], held, drags, repeats, put)
    x[:, dry] = x_in[:, dry]
    y[:, dry] = y_in[:, dry]


def put_fluxes(x_in, y_in, l_in, head, own, x, y, lev, resident, sems):
    rest, top = pl.ds(PACK, l_in.shape[0] - PACK), pl.ds(0, PACK)
    pairs = (
        (x_in, x), (y_in, y), (own, resident.at[0]),
        (l_in.at[rest], lev.at[rest]), (head.at[top], lev.at[top]))
    copies = [pltpu.make_async_copy(source, target, sems.at[i]) for i, (source, target) in enumerate(pairs)]
    for copy in copies:
        copy.start()
    for copy in copies:
        copy.wait()


def put_received(near, far, resident_held, resident, stage, sems):
    copies = []
    for slot, block in enumerate((near, far)):
        stage[slot] = block[...].astype(F32)
        copies.append(pltpu.make_async_copy(stage.at[slot], resident.at[slot + 1], sems.at[slot]))
        copies[-1].start()
    for copy in copies:
        copy.wait()


def add_shares(mine, received, energy):
    shares = mine[...] + received[...]
    lanes = lax.broadcasted_iota(jnp.int32, shares.shape, 1)
    for scenario in range(2):
        energy[scenario] = jnp.sum(jnp.where(lanes % 2 == scenario, shares, 0.0))


def moved(value, steps):
    count = lax.axis_size("tile")
    return lax.ppermute(value, "tile", [(i, (i + steps) % count) for i in range(count)])


def exchange_stages(count):
    deep = 8 if count >= 16 else max(count // 2, 1)
    wide = count // (2 * deep)

    def index(x, z, core):
        return (x * deep + z) * 2 + core

    def stage(rule):
        pairs = []
        for i in range(count):
            core, z, x = i % 2, (i // 2) % deep, i // (2 * deep)
            pairs.append((i, index(*rule(x, z, core))))
        return pairs

    stages = []
    if deep == 8:
        across = {0: 6, 6: 0, 2: 4, 4: 2, 1: 7, 7: 1, 3: 5, 5: 3}
        stages.append(stage(lambda x, z, core: (x, z ^ 2, core)))
        stages.append(stage(lambda x, z, core: (x, across[z], core)))
    if wide >= 2:
        stages.append(stage(lambda x, z, core: (x ^ 1, z, core)))
    if wide == 4:
        stages.append(stage(lambda x, z, core: (3 - x, z, core)))
    stages.append(stage(lambda x, z, core: (x, z, 1 - core)))
    reach = 1
    while reach < (2 if deep == 8 else deep):
        stages.append(stage(lambda x, z, core, reach=reach: (x, z ^ reach, core)))
        reach *= 2
    return stages


def on_device(surface, flux_x, flux_y, celerity, bed_depth, roughness, smoother, plan):
    rows, cols = surface.shape
    side = smoother.shape[0]
    tiles = lax.axis_size("tile")

    def arr(*shape, dtype=F32):
        return jax.ShapeDtypeStruct(shape, dtype)

    field, square = arr(rows, cols), arr(side, side, dtype=BF16)

    def call(body, name, ins, outs, out_specs, operands, scratch=(), aliases={}, flops=0, moved_bytes=0):
        return pl.pallas_call(
            body,
            out_shape=outs,
            in_specs=ins,
            out_specs=out_specs,
            scratch_shapes=scratch,
            input_output_aliases=aliases,
            compiler_params=pltpu.CompilerParams(vmem_limit_bytes=GRANT),
            cost_estimate=pl.CostEstimate(flops=flops, bytes_accessed=moved_bytes, transcendentals=0),
            name=name,
        )(*operands)

    def dots(chains, repeats):
        return chains * repeats * 4 * side**3

    def partner(value, pairs):
        return lax.ppermute(value, "tile", pairs)

    c, b, r, sm = celerity, bed_depth, roughness, smoother
    surface, flux_x, flux_y, celerity = [
        pltpu.with_memory_space_constraint(array, pltpu.HBM)
        for array in (surface, flux_x, flux_y, celerity)
    ]
    drag_shape = arr(rows, cols, dtype=BF16)
    wet_held, wet_drags = arr(3, 2, side, side, dtype=BF16), arr(3, side, side, dtype=BF16)
    up, down, first = call(
        edge_rows, "edge_rows", [HBM] * 4, (arr(5, cols), arr(7, cols), arr(1, cols)), [VMEM] * 3,
        (surface, flux_x, flux_y, celerity),
        [pltpu.VMEM((4, EDGE, cols), F32)] * 2 + [pltpu.SemaphoreType.DMA((8,))])
    up = moved(up, -1)
    down = moved(down, 1)
    x, y, lev, d, sm_t = call(
        first_step, "first_step", [HBM] * 3 + [VMEM] * 4,
        (field, field, field, drag_shape, square), [VMEM] * 5,
        (surface, flux_x, flux_y, c, b, r, sm),
        [pltpu.VMEM((rows, cols), F32)] * 3 + [pltpu.SemaphoreType.DMA((rows // LOAD, 3))],
        flops=20 * rows * cols, moved_bytes=24 * rows * cols)
    held_scratch, drag_scratch = pltpu.VMEM(wet_held.shape, BF16), pltpu.VMEM(wet_drags.shape, BF16)
    x, y, l_head, l_tail, halo, x_last = call(
        lambda *refs: smooth_all(tiles, *refs), "smooth_all", [VMEM] * 13,
        (field, field, arr(EDGE, cols), arr(EDGE, cols), arr(3, cols), arr(1, cols)), [VMEM] * 6,
        (plan, up, down, first, c, b, r, sm, sm_t, x, y, lev, d),
        [held_scratch, drag_scratch, pltpu.VMEM((2 * PACK, cols), BF16), pltpu.VMEM((PACK, cols), F32)],
        flops=dots(6, SUB), moved_bytes=8 * rows * cols)
    down = moved(x_last, 1)
    x, y, lev, d, sums = call(
        lambda *refs: second_step(tiles, *refs), "second_step", [VMEM] * 9,
        (field, field, field, drag_shape, arr(EDGE, cols)), [VMEM] * 5,
        (lev, l_head, l_tail, halo, x, y, c, b, r),
        flops=20 * rows * cols, moved_bytes=8 * rows * cols)
    head, d_head, shares = call(
        lambda *refs: second_edge(tiles, rows, *refs), "second_edge", [VMEM] * 7,
        (arr(PACK, cols), arr(PACK, cols, dtype=BF16), arr(1, 128)), [VMEM] * 3,
        (down, halo, l_head, lev[:PACK], sums, b[:PACK], r[:PACK]), flops=cols, moved_bytes=cols)

    stages = exchange_stages(tiles)
    done = 0

    def exchange(shares, beside):
        nonlocal done
        if done + 1 >= len(stages):
            return (shares,) + tuple(beside())
        met = lax.ppermute(shares, "tile", stages[done])
        done += 1
        return lax.optimization_barrier((shares + met,) + tuple(beside()))

    pair, resident_shape = arr(2, side, side, dtype=BF16), arr(3, 2, side, side)
    shares, held, drags = exchange(shares, lambda: call(
        lambda *refs: start_last(HALF, *refs), "start_last", [VMEM] * 7, (wet_held, wet_drags), [VMEM] * 2,
        (plan, sm, sm_t, x, y, d, d_head), [pltpu.VMEM((PACK, cols), BF16)],
        flops=dots(6, HALF), moved_bytes=rows * cols))
    shares, x, y, own, near, far = exchange(shares, lambda: call(
        lambda *refs: finish_last(SUB - HALF, *refs), "finish_last", [VMEM] * 7,
        (field, field, arr(2, side, side), pair, pair), [VMEM] * 5,
        (plan, sm, sm_t, held, drags, x, y), [held_scratch],
        flops=dots(6, SUB - HALF), moved_bytes=rows * cols))
    far = moved(far, 2)
    shares, x, y, level, resident, near = exchange(shares, lambda: tuple(call(
        put_fluxes, "put_fluxes", [VMEM] * 5, (field, field, field, resident_shape), [HBM] * 4,
        (x, y, lev, head, own), [pltpu.SemaphoreType.DMA((5,))], moved_bytes=16 * rows * cols)) + (near,))
    near = moved(near, 1)
    while done + 1 < len(stages):
        shares, = exchange(shares, tuple)
    met = lax.ppermute(shares, "tile", stages[done])
    resident = call(
        put_received, "put_received", [VMEM] * 2 + [HBM], resident_shape, HBM, (near, far, resident),
        [pltpu.VMEM((2, 2, side, side), F32), pltpu.SemaphoreType.DMA((2,))],
        aliases={2: 0}, moved_bytes=24 * side * side)
    met, resident = lax.optimization_barrier((met, resident))
    energy = call(add_shares, "add_shares", [VMEM] * 2, arr(2), SMEM, (shares, met))
    return level, x, y, resident, energy


def solution(mesh):
    cut = P(("ens", "tile"), None)
    return jax.shard_map(
        on_device,
        mesh=mesh,
        in_specs=(cut,) * 6 + (P(), cut),
        out_specs=(cut, cut, cut, P(("ens", "tile"), None, None, None), P("ens")),
        check_vma=False,
    )
```

```python
import jax
import jax.numpy as jnp
from jax import lax
from jax.experimental import pallas as pl
from jax.experimental.pallas import tpu as pltpu
from jax.sharding import PartitionSpec as P

SUB = 12
HALF = 5
EDGE = 8
PACK = 16
BAND = 32
LOAD = 64
GRANT = 16 * 2**20
F32 = jnp.float32
BF16 = jnp.bfloat16
VMEM = pl.BlockSpec(memory_space=pltpu.VMEM)
SMEM = pl.BlockSpec(memory_space=pltpu.SMEM)
HBM = pl.BlockSpec(memory_space=pltpu.HBM)


def shifted_left(rows, half):
    cols = rows.shape[1]
    ids = lax.broadcasted_iota(jnp.int32, rows.shape, 1) % half
    return jnp.where(ids == half - 1, 0.0, pltpu.roll(rows, cols - 1, 1))


def shifted_right(rows, half):
    ids = lax.broadcasted_iota(jnp.int32, rows.shape, 1) % half
    return jnp.where(ids == 0, 0.0, pltpu.roll(rows, 1, 1))


def drag_of(rough, level, depth):
    return (rough / jnp.maximum(level + depth, 1.0)).astype(BF16)


def code_column(codes, code, side):
    place = lax.broadcasted_iota(jnp.int32, codes.shape, 1) * side
    column = jnp.sum(jnp.where(codes == code, place, 0).astype(F32))
    return pl.multiple_of(column.astype(jnp.int32), side)


def advance(half, level, ahead, flow_x, flow_y, celerity, above_x):
    rows = level.shape[0]
    row_ids = lax.broadcasted_iota(jnp.int32, level.shape, 0)
    below = jnp.where(row_ids == rows - 1, ahead, pltpu.roll(level, rows - 1, 0))
    new_x = flow_x - celerity * (below - level)
    new_y = flow_y - celerity * (shifted_left(level, half) - level)
    behind_x = jnp.where(row_ids == 0, above_x, pltpu.roll(new_x, 1, 0))
    new_level = level - (new_x - behind_x) - (new_y - shifted_right(new_y, half))
    return new_x, new_y, new_level


def edge_rows(s, x, y, c, up, down, first, heads, tails, sems):
    rows = s.shape[0]
    copies = []
    for j, array in enumerate((s, x, y, c)):
        copies.append(pltpu.make_async_copy(array.at[pl.ds(0, EDGE)], heads.at[j], sems.at[2 * j]))
        copies.append(pltpu.make_async_copy(array.at[pl.ds(rows - EDGE, EDGE)], tails.at[j], sems.at[2 * j + 1]))
    for copy in copies:
        copy.start()
    for copy in copies:
        copy.wait()
    up[0:2] = heads[0, 0:2]
    for j in range(1, 4):
        up[j + 1:j + 2] = heads[j, 0:1]
    down[0:2] = tails[0, EDGE - 2:]
    down[2:4] = tails[1, EDGE - 2:]
    down[4:6] = tails[3, EDGE - 2:]
    down[6:7] = tails[2, EDGE - 1:]
    first[...] = heads[0, 0:1]


def first_step(s_in, x_in, y_in, c, b, r, sm, x_out, y_out, l_out, d_out, sm_t, s, x, y, sems):
    total, cols = s.shape
    half = cols // 2
    loads = total // LOAD
    pairs = ((s_in, s), (x_in, x), (y_in, y))

    def copy(i, j):
        rows = pl.ds(i * LOAD, LOAD)
        source, target = pairs[j]
        return pltpu.make_async_copy(source.at[rows], target.at[rows], sems.at[i, j])

    for i in range(loads):
        for j in range(len(pairs)):
            copy(i, j).start()
    sm_t[...] = sm[...].T
    above = jnp.zeros((1, cols), F32)
    for j in range(len(pairs)):
        copy(0, j).wait()
    for i in range(loads):
        if i + 1 < loads:
            for j in range(len(pairs)):
                copy(i + 1, j).wait()
        for start in range(i * LOAD, (i + 1) * LOAD, BAND):
            rows = pl.ds(start, BAND)
            if start + BAND < total:
                ahead = s[pl.ds(start + BAND, 1)]
            else:
                ahead = jnp.zeros((1, cols), F32)
            new_x, new_y, level = advance(half, s[rows], ahead, x[rows], y[rows], c[rows], above)
            above = new_x[BAND - 1:]
            x_out[rows] = new_x
            y_out[rows] = new_y
            l_out[rows] = level
            d_out[rows] = drag_of(r[rows], level, b[rows])


def row_weight(shape, start, total_rows):
    ids = lax.broadcasted_iota(jnp.int32, shape, 0) + start
    return 1.0 + ids.astype(F32) * (2.0 / total_rows)


def second_step(tile_count, l_in, l_head, l_tail, halo, x_in, y_in, c, b, r, x_out, y_out, l_out, d_out, sums_out):
    total, cols = l_in.shape
    half = cols // 2
    bands = total // BAND
    position = lax.axis_index("tile")

    def level_band(i):
        start, stop = i * BAND, (i + 1) * BAND
        parts = [l_in[pl.ds(start, BAND)]]
        if i == 0:
            parts = [l_head[...], l_in[pl.ds(EDGE, BAND - EDGE)]]
        if i == bands - 1:
            parts = [l_in[pl.ds(start, BAND - EDGE)], l_tail[...]]
        return jnp.concatenate(parts, 0)

    above = jnp.zeros((1, cols), F32)
    sums = jnp.zeros((EDGE, cols), F32)
    level = level_band(0)
    for i in range(bands):
        rows = pl.ds(i * BAND, BAND)
        following = level_band(i + 1) if i + 1 < bands else halo[...]
        new_x, new_y, new_level = advance(half, level, following[0:1], x_in[rows], y_in[rows], c[rows], above)
        level = following
        above = new_x[BAND - 1:]
        x_out[rows] = new_x
        y_out[rows] = new_y
        l_out[rows] = new_level
        d_out[rows] = drag_of(r[rows], new_level, b[rows])
        for j in range(BAND // EDGE):
            if i + j > 0:
                part = new_level[j * EDGE:(j + 1) * EDGE]
                weight = row_weight(part.shape, position * total + i * BAND + j * EDGE, tile_count * total)
                sums = sums + weight * (part * part)
    sums_out[...] = sums


def second_edge(tile_count, row_count, down, halo, l_head, l2_head, sums, b_head, r_head, head, d_head, shares):
    cols = l_head.shape[1]
    half = cols // 2
    position = lax.axis_index("tile")
    total_rows = tile_count * row_count
    has_previous = jnp.where(position == 0, 0.0, 1.0)
    above_x = has_previous * (down[...] - halo[2:3] * (l_head[0:1] - halo[1:2]))
    row_ids = lax.broadcasted_iota(jnp.int32, (PACK, cols), 0)
    level = l2_head[...] + jnp.where(row_ids == 0, above_x, 0.0)
    head[...] = level
    d_head[...] = drag_of(r_head[...], level, b_head[...])
    top = level[:EDGE]
    whole = sums[...] + row_weight(top.shape, position * row_count, total_rows) * (top * top)
    lanes = lax.broadcasted_iota(jnp.int32, (1, 128), 1)
    share = jnp.zeros((1, 128), F32)
    for scenario in range(2):
        part = whole[:, scenario * half:(scenario + 1) * half]
        share = jnp.where(lanes == 2 * position + scenario, jnp.sum(part) * (1.0 / (total_rows * half)), share)
    shares[...] = share


def soften(smooth, smooth_t, source, held, drags, repeats, put=None):
    for repeat in range(repeats):
        for slot in range(drags.shape[0]):
            for f in range(2):
                block = source(slot, f) if repeat == 0 else held[slot, f]
                mixed = jnp.dot(block, smooth_t, preferred_element_type=F32).astype(BF16)
                full = jnp.dot(smooth, mixed, preferred_element_type=F32)
                settled = full / (1.0 + drags[slot].astype(F32) * jnp.abs(full))
                if put is None or repeat + 1 < repeats:
                    held[slot, f] = settled.astype(BF16)
                else:
                    put(slot, f, settled)


def smooth_all(tile_count, plan, up, down, first, c, b, r, sm, sm_t, x_in, y_in, l_in, d_in,
               x, y, l_head, l_tail, halo, x_last, held, drags, edge, low_x):
    rows, cols = x.shape
    half = cols // 2
    side = sm.shape[0]
    position = lax.axis_index("tile")
    has_next = jnp.where(position == tile_count - 1, 0.0, 1.0)
    has_previous = jnp.where(position == 0, 0.0, 1.0)
    below = up[...] * has_next
    above = down[...] * has_previous
    tail, head = pl.ds(rows - EDGE, EDGE), pl.ds(0, EDGE)
    row_ids = lax.broadcasted_iota(jnp.int32, (EDGE, cols), 0)
    own_first = first[...]

    change = jnp.where(row_ids == EDGE - 1, c[tail] * below[0:1], 0.0)
    x_tail = x_in[tail] - change
    low_x[0:EDGE] = x_in[pl.ds(rows - PACK, EDGE)]
    low_x[EDGE:PACK] = x_tail
    low = l_in[tail] + change
    l_tail[...] = low
    above_x = above[3:4] - above[5:6] * (own_first - above[1:2])
    top = l_in[head] + jnp.where(row_ids == 0, above_x, 0.0)
    l_head[...] = top

    next_x = below[2:3] - below[4:5] * (below[1:2] - below[0:1])
    next_y = below[3:4] - below[4:5] * (shifted_left(below[0:1], half) - below[0:1])
    next_level = below[0:1] - (next_x - x_tail[EDGE - 1:]) - (next_y - shifted_right(next_y, half))
    halo[0:1] = has_next * next_level
    before_x = above[2:3] - above[4:5] * (above[1:2] - above[0:1])
    before_y = above[6:7] - above[5:6] * (shifted_left(above[1:2], half) - above[1:2])
    halo[1:2] = above[1:2] - (above_x - before_x) - (before_y - shifted_right(before_y, half))
    halo[2:3] = above[5:6]

    first_rows, last_rows = pl.ds(0, PACK), pl.ds(rows - PACK, PACK)
    first_edge, last_edge = pl.ds(0, PACK), pl.ds(PACK, PACK)
    edge[first_edge] = drag_of(r[first_rows], jnp.concatenate([top, l_in[pl.ds(EDGE, EDGE)]], 0), b[first_rows])
    edge[last_edge] = drag_of(r[last_rows], jnp.concatenate([l_in[pl.ds(rows - PACK, EDGE)], low], 0), b[last_rows])
    codes = plan[...]
    dry = pl.ds(code_column(codes, 0, side), side)
    x[:, dry] = x_in[:, dry]
    x[last_rows, dry] = low_x[:, dry]
    y[:, dry] = y_in[:, dry]
    columns = [code_column(codes, code, side) for code in (1, 2, 3)]
    for slot, column in enumerate(columns):
        span = pl.ds(column, side)
        drags[slot] = d_in[:, span]
        drags[slot, first_rows] = edge[first_edge, span]
        drags[slot, last_rows] = edge[last_edge, span]
        held[slot, 0] = x_in[:, span].astype(BF16)
        held[slot, 0, last_rows] = low_x[:, span].astype(BF16)
        held[slot, 1] = y_in[:, span].astype(BF16)

    def put(slot, f, settled):
        (x, y)[f][:, pl.ds(columns[slot], side)] = settled

    soften(sm[...], sm_t[...], lambda slot, f: held[slot, f], held, drags, SUB, put)
    x_last[...] = x[rows - 1:rows]


def start_last(repeats, plan, sm, sm_t, x, y, d, d_head, held, drags, edge):
    side = sm.shape[0]
    codes = plan[...]
    edge[...] = d_head[...]
    spans = [pl.ds(code_column(codes, code, side), side) for code in (1, 2, 3)]
    for slot, span in enumerate(spans):
        drags[slot] = d[:, span]
        drags[slot, 0:PACK] = edge[:, span]
    soften(sm[...], sm_t[...], lambda slot, f: (x, y)[f][:, spans[slot]].astype(BF16), held, drags, repeats)


def finish_last(repeats, plan, sm, sm_t, held_in, drags, x_in, y_in, x, y, own, near, far, held):
    side = sm.shape[0]
    codes = plan[...]
    dry, *spans = [pl.ds(code_column(codes, code, side), side) for code in range(4)]

    def put(slot, f, settled):
        (x, y)[f][:, spans[slot]] = settled
        if slot == 0:
            own[f] = settled
        else:
            (near, far)[slot - 1][f] = settled.astype(BF16)

    soften(sm[...], sm_t[...], lambda slot, f: held_in[slot, f], held, drags, repeats, put)
    x[:, dry] = x_in[:, dry]
    y[:, dry] = y_in[:, dry]


def put_fluxes(x_in, y_in, l_in, head, own, x, y, lev, resident, sems):
    rest, top = pl.ds(PACK, l_in.shape[0] - PACK), pl.ds(0, PACK)
    pairs = (
        (x_in, x), (y_in, y), (own, resident.at[0]),
        (l_in.at[rest], lev.at[rest]), (head.at[top], lev.at[top]))
    copies = [pltpu.make_async_copy(source, target, sems.at[i]) for i, (source, target) in enumerate(pairs)]
    for copy in copies:
        copy.start()
    for copy in copies:
        copy.wait()


def put_received(near, far, resident_held, resident, stage, sems):
    copies = []
    for slot, block in enumerate((near, far)):
        stage[slot] = block[...].astype(F32)
        copies.append(pltpu.make_async_copy(stage.at[slot], resident.at[slot + 1], sems.at[slot]))
        copies[-1].start()
    for copy in copies:
        copy.wait()


def add_shares(mine, received, energy):
    shares = mine[...] + received[...]
    lanes = lax.broadcasted_iota(jnp.int32, shares.shape, 1)
    for scenario in range(2):
        energy[scenario] = jnp.sum(jnp.where(lanes % 2 == scenario, shares, 0.0))


def moved(value, steps):
    count = lax.axis_size("tile")
    return lax.ppermute(value, "tile", [(i, (i + steps) % count) for i in range(count)])


def exchange_stages(count):
    deep = 8 if count >= 16 else max(count // 2, 1)
    wide = count // (2 * deep)

    def index(x, z, core):
        return (x * deep + z) * 2 + core

    def stage(rule):
        pairs = []
        for i in range(count):
            core, z, x = i % 2, (i // 2) % deep, i // (2 * deep)
            pairs.append((i, index(*rule(x, z, core))))
        return pairs

    stages = []
    if deep == 8:
        across = {0: 6, 6: 0, 2: 4, 4: 2, 1: 7, 7: 1, 3: 5, 5: 3}
        stages.append(stage(lambda x, z, core: (x, z ^ 2, core)))
        stages.append(stage(lambda x, z, core: (x, across[z], core)))
    if wide >= 2:
        stages.append(stage(lambda x, z, core: (x ^ 1, z, core)))
    if wide == 4:
        stages.append(stage(lambda x, z, core: (3 - x, z, core)))
    stages.append(stage(lambda x, z, core: (x, z, 1 - core)))
    reach = 1
    while reach < (2 if deep == 8 else deep):
        stages.append(stage(lambda x, z, core, reach=reach: (x, z ^ reach, core)))
        reach *= 2
    return stages


def on_device(surface, flux_x, flux_y, celerity, bed_depth, roughness, smoother, plan):
    rows, cols = surface.shape
    side = smoother.shape[0]
    tiles = lax.axis_size("tile")

    def arr(*shape, dtype=F32):
        return jax.ShapeDtypeStruct(shape, dtype)

    field, square = arr(rows, cols), arr(side, side, dtype=BF16)

    def call(body, name, ins, outs, out_specs, operands, scratch=(), aliases={}, flops=0, moved_bytes=0):
        return pl.pallas_call(
            body,
            out_shape=outs,
            in_specs=ins,
            out_specs=out_specs,
            scratch_shapes=scratch,
            input_output_aliases=aliases,
            compiler_params=pltpu.CompilerParams(vmem_limit_bytes=GRANT),
            cost_estimate=pl.CostEstimate(flops=flops, bytes_accessed=moved_bytes, transcendentals=0),
            name=name,
        )(*operands)

    def dots(chains, repeats):
        return chains * repeats * 4 * side**3

    def partner(value, pairs):
        return lax.ppermute(value, "tile", pairs)

    c, b, r, sm = celerity, bed_depth, roughness, smoother
    surface, flux_x, flux_y, celerity = [
        pltpu.with_memory_space_constraint(array, pltpu.HBM)
        for array in (surface, flux_x, flux_y, celerity)
    ]
    drag_shape = arr(rows, cols, dtype=BF16)
    wet_held, wet_drags = arr(3, 2, side, side, dtype=BF16), arr(3, side, side, dtype=BF16)
    up, down, first = call(
        edge_rows, "edge_rows", [HBM] * 4, (arr(5, cols), arr(7, cols), arr(1, cols)), [VMEM] * 3,
        (surface, flux_x, flux_y, celerity),
        [pltpu.VMEM((4, EDGE, cols), F32)] * 2 + [pltpu.SemaphoreType.DMA((8,))])
    up = moved(up, -1)
    down = moved(down, 1)
    x, y, lev, d, sm_t = call(
        first_step, "first_step", [HBM] * 3 + [VMEM] * 4,
        (field, field, field, drag_shape, square), [VMEM] * 5,
        (surface, flux_x, flux_y, c, b, r, sm),
        [pltpu.VMEM((rows, cols), F32)] * 3 + [pltpu.SemaphoreType.DMA((rows // LOAD, 3))],
        flops=20 * rows * cols, moved_bytes=24 * rows * cols)
    held_scratch, drag_scratch = pltpu.VMEM(wet_held.shape, BF16), pltpu.VMEM(wet_drags.shape, BF16)
    x, y, l_head, l_tail, halo, x_last = call(
        lambda *refs: smooth_all(tiles, *refs), "smooth_all", [VMEM] * 13,
        (field, field, arr(EDGE, cols), arr(EDGE, cols), arr(3, cols), arr(1, cols)), [VMEM] * 6,
        (plan, up, down, first, c, b, r, sm, sm_t, x, y, lev, d),
        [held_scratch, drag_scratch, pltpu.VMEM((2 * PACK, cols), BF16), pltpu.VMEM((PACK, cols), F32)],
        flops=dots(6, SUB), moved_bytes=8 * rows * cols)
    down = moved(x_last, 1)
    x, y, lev, d, sums = call(
        lambda *refs: second_step(tiles, *refs), "second_step", [VMEM] * 9,
        (field, field, field, drag_shape, arr(EDGE, cols)), [VMEM] * 5,
        (lev, l_head, l_tail, halo, x, y, c, b, r),
        flops=20 * rows * cols, moved_bytes=8 * rows * cols)
    head, d_head, shares = call(
        lambda *refs: second_edge(tiles, rows, *refs), "second_edge", [VMEM] * 7,
        (arr(PACK, cols), arr(PACK, cols, dtype=BF16), arr(1, 128)), [VMEM] * 3,
        (down, halo, l_head, lev[:PACK], sums, b[:PACK], r[:PACK]), flops=cols, moved_bytes=cols)

    stages = exchange_stages(tiles)
    done = 0

    def exchange(shares, beside):
        nonlocal done
        if done + 1 >= len(stages):
            return (shares,) + tuple(beside())
        met = lax.ppermute(shares, "tile", stages[done])
        done += 1
        return lax.optimization_barrier((shares + met,) + tuple(beside()))

    pair, resident_shape = arr(2, side, side, dtype=BF16), arr(3, 2, side, side)
    shares, held, drags = exchange(shares, lambda: call(
        lambda *refs: start_last(HALF, *refs), "start_last", [VMEM] * 7, (wet_held, wet_drags), [VMEM] * 2,
        (plan, sm, sm_t, x, y, d, d_head), [pltpu.VMEM((PACK, cols), BF16)],
        flops=dots(6, HALF), moved_bytes=rows * cols))
    shares, x, y, own, near, far = exchange(shares, lambda: call(
        lambda *refs: finish_last(SUB - HALF, *refs), "finish_last", [VMEM] * 7,
        (field, field, arr(2, side, side), pair, pair), [VMEM] * 5,
        (plan, sm, sm_t, held, drags, x, y), [held_scratch],
        flops=dots(6, SUB - HALF), moved_bytes=rows * cols))
    far = moved(far, 2)
    shares, x, y, level, resident, near = exchange(shares, lambda: tuple(call(
        put_fluxes, "put_fluxes", [VMEM] * 5, (field, field, field, resident_shape), [HBM] * 4,
        (x, y, lev, head, own), [pltpu.SemaphoreType.DMA((5,))], moved_bytes=16 * rows * cols)) + (near,))
    near = moved(near, 1)
    while done + 1 < len(stages):
        shares, = exchange(shares, tuple)
    met = lax.ppermute(shares, "tile", stages[done])
    resident = call(
        put_received, "put_received", [VMEM] * 2 + [HBM], resident_shape, HBM, (near, far, resident),
        [pltpu.VMEM((2, 2, side, side), F32), pltpu.SemaphoreType.DMA((2,))],
        aliases={2: 0}, moved_bytes=24 * side * side)
    met, resident = lax.optimization_barrier((met, resident))
    energy = call(add_shares, "add_shares", [VMEM] * 2, arr(2), SMEM, (shares, met))
    return level, x, y, resident, energy


def solution(mesh):
    cut = P(("ens", "tile"), None)
    return jax.shard_map(
        on_device,
        mesh=mesh,
        in_specs=(cut,) * 6 + (P(), cut),
        out_specs=(cut, cut, cut, P(("ens", "tile"), None, None, None), P("ens")),
        check_vma=False,
    )
```
